32 devices in a mesh: row: 4 (over y, x), col: 8 (over z, core).
Axes of the slice: x: 2, y: 2, z: 4, core: 2. Of those that a mesh axis runs over, the one named last changes fastest.
Arguments:
- top_coeffs: float32 [8, 32768], P(None, ('row', 'col')), may hold values from -6 to 6
- fresh_one: bfloat16 [56, 32768], P(None, ('row', 'col')), may hold values from -6 to 6
- fresh_two: bfloat16 [56, 8, 32768], P(None, None, ('row', 'col')), may hold values from -6 to 6
- fresh_three: bfloat16 [56, 64, 32768], P(None, None, ('row', 'col')), may hold values from -6 to 6
- mixing: bfloat16 [64, 64], replicated, may hold values from -0.75 to 0.75
- transfer: float32 [1024, 1024], P(None, 'col'), may hold values from 0.1 to 1, as said below
Outputs:
- density: float32 [16, 1024, 1024], P('row', 'col')
The draws below stay inside these ranges and needn't reach their ends.
Inputs may be any that keep to these rules, and one draw needn't show every extreme that they name: transfer is even: its value at the positions of modes (ky, kz) equals its value at the positions of modes (-ky mod 1024, -kz mod 1024).
All inputs are finite; a program needn't handle non-finite values.
Results may differ from the reference program's by a relative error of at most 0.0003.
Values sent between devices are 32-bit elements; how exact they have to be, the bound alone decides.
No kernel may reach another device: no remote copies, remote signals or barrier semaphores. Data moves between devices by JAX's collectives and lax.ppermute only.
A program may use at most 192 MiB of HBM per device.

```python
import math
import jax
import jax.numpy as jnp
import numpy as np
from jax import lax

NG = 1024
PLANES = 16
BLOCKS = 128
NBLK = 32768
SLOTS = 1024
N_ROW = 4
N_COL = 8


def draw_transfer(key, part):
    base = jnp.exp(jax.random.uniform(key, (NG, NG), jnp.float32, math.log(0.1), 0.0))
    mirrored = jnp.roll(base[::-1, ::-1], (1, 1), axis=(0, 1))
    natural = 0.5 * (base + mirrored)
    major = NG // 128
    return natural.reshape(128, major, 128, major).transpose(1, 0, 3, 2).reshape(NG, NG).astype(jnp.float32)


def level_of(own_key, shape, pieces, smallest, high):
    def one(position, blocks):
        draws = jax.random.uniform(jax.random.fold_in(jax.random.fold_in(own_key, 6), position), (blocks,), jnp.float32, smallest / len(pieces), high / len(pieces))
        return jnp.repeat(jnp.exp(draws), shape[position] // blocks).reshape((-1,) + (1,) * (len(shape) - position - 1))

    level = one(*pieces[0])
    for cut in pieces[1:]:
        level = level * one(*cut)
    return level


def bell_draw(own_key, shape, scale, limit, split=(), held_as=jnp.bfloat16):
    values = scale * jax.random.normal(own_key, shape, jnp.float32)
    if split:
        values = values * level_of(own_key, shape, split, -0.22, 0.18)
    return jnp.clip(values, -limit, limit).astype(held_as)


def setup_inputs(seed: int = 0) -> dict:
    keys = jax.random.split(jax.random.key(seed), 7)
    return {
        "top_coeffs": bell_draw(keys[0], (8, NBLK), 1.0, 6.0, ((1, 32),), jnp.float32),
        "fresh_one": bell_draw(keys[1], (56, NBLK), 1.0, 6.0, ((1, 32),)),
        "fresh_two": bell_draw(keys[2], (56, 8, NBLK), 1.0, 6.0, ((2, 32),)),
        "fresh_three": bell_draw(keys[3], (56, 64, NBLK), 1.0, 6.0, ((2, 32),)),
        "mixing": bell_draw(keys[4], (64, 64), 64 ** -0.5, 0.75),
        "transfer": draw_transfer(jax.random.fold_in(keys[6], 71), 0),
    }


def expand_level(parents, fresh, mixing, full):
    rows = mixing if full else mixing[0::8]
    count = rows.shape[0]
    cells = parents.shape[1]
    blocks = parents.shape[2]
    carried = jnp.einsum("ij,jcb->icb", rows[:, :8].astype(jnp.float32), parents, precision=lax.Precision.HIGHEST)
    drawn = jnp.einsum("ij,jcb->icb", rows[:, 8:].astype(jnp.float32), fresh.astype(jnp.float32), precision=lax.Precision.HIGHEST)
    total = carried + drawn
    if full:
        return total.reshape(8, 8, cells, blocks).transpose(1, 2, 0, 3).reshape(8, cells * 8, blocks)
    return total.transpose(1, 0, 2).reshape(cells * 8, blocks)


def record_table(block_count, n_row, n_col):
    owners = n_row * n_col
    per_strip = block_count // n_col
    y_bits = per_strip.bit_length() - 1
    class_slots = per_strip * block_count // owners
    slot_count = 2 * n_col * class_slots
    x_half, y_block, z_block = np.meshgrid(np.arange(2), np.arange(block_count), np.arange(block_count), indexing="ij")
    strip = y_block // per_strip
    y_local = y_block % per_strip
    code = z_block * 0
    for bit_index in range(y_bits):
        code = code + (((z_block >> bit_index) & 1) << (2 * bit_index))
        code = code + (((y_local >> bit_index) & 1) << (2 * bit_index + 1))
    code = code + ((z_block >> y_bits) << (2 * y_bits))
    owner = code % owners
    inner = code // owners
    record = owner * slot_count + (x_half * n_col + strip) * class_slots + inner
    return record.astype(np.int32)


def reference(top_coeffs, fresh_one, fresh_two, fresh_three, mixing, transfer):
    owners = N_ROW * N_COL

    def leaves_of(index):
        start = index * SLOTS
        top = lax.dynamic_slice_in_dim(top_coeffs, start, SLOTS, 1)
        first = lax.dynamic_slice_in_dim(fresh_one, start, SLOTS, 1)
        second = lax.dynamic_slice_in_dim(fresh_two, start, SLOTS, 2)
        third = lax.dynamic_slice_in_dim(fresh_three, start, SLOTS, 2)
        level = expand_level(top[:, None, :], first[:, None, :], mixing, True)
        level = expand_level(level, second, mixing, True)
        return expand_level(level, third, mixing, False)

    leaves = lax.map(leaves_of, jnp.arange(owners, dtype=jnp.int32))
    records = leaves.transpose(0, 2, 1).reshape(NBLK, 512)
    table = jnp.asarray(record_table(BLOCKS, N_ROW, N_COL)).astype(jnp.int32)
    grid = jnp.take(records, table, axis=0)
    grid = grid.reshape((2, BLOCKS, BLOCKS) + (2,) * 9)
    field = grid.transpose(0, 3, 6, 9, 1, 4, 7, 10, 2, 5, 8, 11).reshape(PLANES, NG, NG)
    spectrum = jnp.fft.fft2(field, axes=(1, 2))
    major = NG // 128
    natural = transfer.reshape(major, 128, major, 128).transpose(1, 0, 3, 2).reshape(NG, NG)
    result = jnp.fft.ifft2(spectrum * natural, axes=(1, 2))
    return jnp.real(result).astype(jnp.float32)
```

```python
import functools
import math

import jax
import jax.numpy as jnp
import numpy as np
from jax import lax
from jax.experimental import pallas as pl
from jax.experimental.pallas import tpu as pltpu
from jax.sharding import PartitionSpec as P

F32 = jnp.float32
BF16 = jnp.bfloat16
LANES = 128
VMEM_LIMIT = 60 * 1024 * 1024


def bits_of(count):
    return count.bit_length() - 1


class Plan:
    def __init__(self, n_row, n_col, slots, grid):
        self.n_row, self.n_col, self.slots, self.grid = n_row, n_col, slots, grid
        self.owners = n_row * n_col
        self.planes = 16 // n_row
        self.pairs = self.planes // 2
        self.dest_x = n_row // 2
        self.blocks = grid // 8
        self.strip = self.blocks // n_col
        self.inner = slots // (2 * n_col)
        self.major = grid // LANES
        self.quarter = grid // 4
        own_bits = bits_of(self.owners)
        self.own_w = [k for k in range(own_bits) if k % 2 == 0]
        self.own_q = [k for k in range(own_bits) if k % 2 == 1]
        y_bits, z_bits = bits_of(self.strip), bits_of(self.blocks)
        code = []
        for k in range(y_bits):
            code += [("w", k), ("q", k)]
        code += [("w", k) for k in range(y_bits, z_bits)]
        self.inner_bits = code[own_bits:]
        top = bits_of(n_col)
        self.top_w = list(range(z_bits - top, z_bits))
        self.q_in = [k for kind, k in self.inner_bits if kind == "q"]
        self.mid_w = [k for kind, k in self.inner_bits if kind == "w" and k not in self.top_w]
        self.t_low = bits_of(LANES // self.inner)
        self.w_kept = 2 ** len(self.mid_w)
        self.rows_rw = 2 * self.w_kept
        self.small = 2 ** (self.t_low + len(self.q_in))
        assert self.small == 8 and n_col == self.major and slots // 2 == 4 * LANES
        self.src_rows = self.rows_rw * 2 * self.small
        self.q_stack = LANES // self.src_rows
        self.q_rest = 2 ** len(self.own_q) // self.q_stack
        self.w_extra = 2 ** len(self.own_w) // 8
        assert self.w_extra * self.w_kept == 2

    def send_table(self):
        lane = np.arange(LANES)
        low_t, inner = lane // self.inner, lane % self.inner
        top = np.zeros(LANES, np.int64)
        small = low_t.copy()
        kept = np.zeros(LANES, np.int64)
        q_value = np.zeros(LANES, np.int64)
        for place, (kind, k) in enumerate(self.inner_bits):
            bit = (inner >> place) & 1
            if kind == "q":
                q_value += bit << self.q_in.index(k)
            elif k in self.top_w:
                top += bit << self.top_w.index(k)
            else:
                kept += bit << self.mid_w.index(k)
        small = (low_t << len(self.q_in)) + q_value
        table = np.zeros((self.n_col, 2, self.w_kept, self.small, 2, LANES))
        for c in range(self.n_col):
            angle = 2 * np.pi * (c * top % self.n_col) / self.n_col
            cos, sin = np.cos(angle), np.sin(angle)
            table[c, 0, kept, small, 0, lane] = cos
            table[c, 0, kept, small, 1, lane] = sin
            table[c, 1, kept, small, 0, lane] = -sin
            table[c, 1, kept, small, 1, lane] = cos
        return table.reshape(self.n_col * self.rows_rw * self.small, 2 * LANES)

    def lane_z(self):
        lane = np.arange(LANES)
        return (lane >> 4) * 8 + ((lane >> 3) & 1) * 4 + (lane & 3), (lane >> 2) & 1

    def z_table(self):
        low, y_bit = self.lane_z()
        k = np.arange(LANES)
        table = np.zeros((2, 2, LANES, 2, 2, LANES))
        for kept in range(2):
            phase = np.outer(64 * kept + low, k) % LANES
            cos, sin = np.cos(2 * np.pi * phase / LANES), np.sin(2 * np.pi * phase / LANES)
            for b in range(2):
                mask = (y_bit == b)[:, None]
                table[kept, 0, :, b, 0] = cos * mask
                table[kept, 1, :, b, 0] = sin * mask
                table[kept, 0, :, b, 1] = -sin * mask
                table[kept, 1, :, b, 1] = cos * mask
        return table.reshape(4 * LANES, 4 * LANES)

    def y_rows(self):
        shape = (2, self.q_rest, 4, self.q_stack, self.small)
        y0, q_rest, y21, q_stack, small = np.indices(shape)
        n_in = len(self.q_in)
        t_low, q_in = small >> n_in, small & (2 ** n_in - 1)
        q_local = q_in * 2 ** len(self.own_q) + q_rest * self.q_stack + q_stack
        return (t_low * LANES + q_local * 8 + y21 * 2 + y0).reshape(-1)

    def m_rows(self):
        step = self.major // 4
        return (np.arange(step)[:, None] + step * np.arange(LANES)[None, :]).reshape(-1)

    def y_tables(self):
        n2, m, size = self.y_rows(), self.m_rows(), self.quarter
        angle = 2 * np.pi * (np.outer(m, n2) % size) / size
        cos, sin = np.cos(angle), np.sin(angle)
        ahead = np.block([[cos, sin], [-sin, cos]])
        angle = 2 * np.pi * (np.outer(np.arange(size), m) % size) / size
        cos, sin = np.cos(angle), np.sin(angle)
        return ahead, np.block([[cos, -sin], [sin, cos]])

    def turns(self):
        out = np.zeros((2, self.quarter, LANES), np.float32)
        for order, n2 in enumerate((self.y_rows(), np.arange(self.quarter))):
            for j in range(4):
                angle = 2 * np.pi * (n2 * j) / self.grid
                out[order, :, j] = np.cos(angle)
                out[order, :, 8 + j] = np.sin(angle)
        return out

    def z_back(self):
        n = np.arange(LANES)
        angle = 2 * np.pi * (np.outer(n, n) % LANES) / LANES
        cos, sin = np.cos(angle), np.sin(angle)
        return np.block([[cos, sin], [-sin, cos]])

    def src(self, w, q):
        index = 0
        for place, bit in enumerate(self.own_w):
            index |= ((w >> place) & 1) << bit
        for place, bit in enumerate(self.own_q):
            index |= ((q >> place) & 1) << bit
        return index


def halves(table):
    high = np.asarray(table, np.float32).astype(BF16)
    low = (np.asarray(table, np.float64) - high.astype(np.float64)).astype(BF16)
    return np.stack((high, low))


def split(x):
    high = x.astype(BF16)
    return high, (x - high.astype(F32)).astype(BF16)


def dot(a, b):
    return jnp.dot(a, b, preferred_element_type=F32)


def dot_nt(a, b):
    return lax.dot_general(a, b, (((1,), (1,)), ((), ())), preferred_element_type=F32)


def three(f, a, b):
    return f(a[0], b[0]) + (f(a[0], b[1]) + f(a[1], b[0]))


def one_hot(shape, hit):
    row = lax.broadcasted_iota(jnp.int32, shape, 0)
    col = lax.broadcasted_iota(jnp.int32, shape, 1)
    return jnp.where(hit(row, col), 1.0, 0.0).astype(BF16)


def spread(mixing, rows, row_of, same, fresh):
    pick = one_hot((rows, 64), lambda r, c: c == row_of(r))
    if fresh:
        wide = one_hot((64, 448), lambda r, c: r == 8 + c // 8)
        cell = lambda c: c % 8
    else:
        wide = one_hot((64, 64), lambda r, c: r == c % 8)
        cell = lambda c: c // 8
    table = dot(dot(pick, mixing).astype(BF16), wide)
    row = lax.broadcasted_iota(jnp.int32, table.shape, 0)
    col = lax.broadcasted_iota(jnp.int32, table.shape, 1)
    return jnp.where(same(row) == cell(col), table, 0.0).astype(BF16)


def carry(table, parents):
    high = parents.astype(BF16)
    rest = parents - high.astype(F32)
    mid = rest.astype(BF16)
    low = (rest - mid.astype(F32)).astype(BF16)
    return dot(table, high) + (dot(table, mid) + dot(table, low))


def expand_kernel(plan, top, one, two, three_ref, mixing, send, *refs):
    outs = refs[: plan.pairs]
    leaf, w2f, w2p, w3f, w3p = refs[plan.pairs :]

    @pl.when(pl.program_id(0) == 0)
    def _():
        mix = mixing[...]
        w2f[...] = spread(mix, 512, lambda r: r % 64, lambda r: r // 64, True)
        w2p[...] = spread(mix, 512, lambda r: r % 64, lambda r: r // 64, False)
        child = lambda r: 8 * (4 * (r // 32 % 2) + 2 * (r // 4 % 2) + r % 2)
        cell = lambda r: 4 * (r // 16 % 2) + 2 * (r // 8 % 2) + r // 2 % 2
        w3f[...] = spread(mix, 64, child, cell, True)
        w3p[...] = spread(mix, 64, child, cell, False)

    mix = mixing[...]
    level = carry(mix[:, :8], top[...]) + dot(mix[:, 8:], one[...])
    for g in range(8):
        rows = pl.ds(64 * g, 64)
        second = dot(w2f[rows, :], two[...]) + carry(w2p[rows, :], level)
        fresh = three_ref[:, pl.ds(8 * g, 8), :].reshape(448, second.shape[1])
        leaf[g] = dot(w3f[...], fresh) + carry(w3p[...], second)
    table = (send[0], send[1])
    for x in range(4):
        x2, x1 = x // 2, x % 2
        pair, dest = x % plan.pairs, x // plan.pairs
        for high in range(2):
            parts = []
            for part in range(2):
                pieces = [
                    leaf[4 * x2 + yz, pl.ds(32 * part + 16 * x1, 16), pl.ds((2 * high + tau) * LANES, LANES)]
                    for tau in range(2)
                    for yz in range(4)
                ]
                parts.append(jnp.concatenate(pieces, axis=0))
            data = split(jnp.concatenate(parts, axis=1))
            sent = three(dot_nt, table, data)
            outs[pair][0, dest, :, :, high] = sent.reshape(plan.n_col, plan.rows_rw, plan.small, LANES)


def expand(plan, top, one, two, three_in, mixing):
    half = plan.slots // 2
    shape = (2, plan.dest_x, plan.n_col, plan.rows_rw, 2, plan.small, LANES)
    table = halves(plan.send_table())
    whole = lambda array: pl.BlockSpec(array.shape, lambda i: (0,) * array.ndim)
    return pl.pallas_call(
        functools.partial(expand_kernel, plan),
        grid=(2,),
        in_specs=[
            pl.BlockSpec((8, half), lambda i: (0, i)),
            pl.BlockSpec((56, half), lambda i: (0, i)),
            pl.BlockSpec((448, half), lambda i: (0, i)),
            pl.BlockSpec((56, 64, half), lambda i: (0, 0, i)),
            whole(mixing),
            whole(table),
        ],
        out_specs=[pl.BlockSpec((1,) + shape[1:], lambda i: (i, 0, 0, 0, 0, 0, 0))] * plan.pairs,
        out_shape=[jax.ShapeDtypeStruct(shape, F32)] * plan.pairs,
        scratch_shapes=[
            pltpu.VMEM((8, 64, half), F32),
            pltpu.VMEM((512, 448), BF16),
            pltpu.VMEM((512, 64), BF16),
            pltpu.VMEM((64, 448), BF16),
            pltpu.VMEM((64, 64), BF16),
        ],
        compiler_params=pltpu.CompilerParams(vmem_limit_bytes=VMEM_LIMIT),
        name="expand",
    )(top, one, two.reshape(448, plan.slots), three_in, mixing, jnp.asarray(table))


def dft4(parts, sign):
    (ar, ai), (br, bi), (cr, ci), (dr, di) = parts
    pr, pi, mr, mi = ar + cr, ai + ci, ar - cr, ai - ci
    qr, qi, nr, ni = br + dr, bi + di, br - dr, bi - di
    return [
        (pr + qr, pi + qi),
        (mr - sign * ni, mi + sign * nr),
        (pr - qr, pi - qi),
        (mr + sign * ni, mi - sign * nr),
    ]


def middle_kernel(plan, got, factor, lane_turn, z_in, y_in, y_out, turns, z_out, out, flipped, prep):
    q_tiles = plan.q_rest * 4 * plan.q_stack
    for q_rest in range(plan.q_rest):
        for extra in range(plan.w_extra):
            for w in range(8):
                stack = [
                    got[plan.src(extra * 8 + w, q_rest * plan.q_stack + q)].reshape(plan.src_rows, LANES)
                    for q in range(plan.q_stack)
                ]
                flipped[w] = jnp.concatenate(stack, axis=0).T.reshape(16, 8, LANES)
            for tau in range(2):
                for y21 in range(4):
                    y2, y1 = y21 // 2, y21 % 2
                    pieces = [
                        flipped[w, 8 * tau + 4 * y2 + 2 * z2 + y1] for w in range(8) for z2 in range(2)
                    ]
                    block = jnp.concatenate(pieces, axis=0).T
                    block = block.reshape(plan.q_stack, 2, plan.w_kept, 2, 8, LANES)
                    for kept_in in range(plan.w_kept):
                        kept = extra if plan.w_extra == 2 else kept_in
                        cos = lane_turn[2 * kept : 2 * kept + 1, :]
                        sin = lane_turn[2 * kept + 1 : 2 * kept + 2, :]
                        for q in range(plan.q_stack):
                            for high in range(2):
                                re, im = block[q, 0, kept_in, high], block[q, 1, kept_in, high]
                                tile = (2 * high + tau) * q_tiles + (q_rest * 4 + y21) * plan.q_stack + q
                                rows = pl.ds(8 * tile, 8)
                                prep[rows, pl.ds(2 * kept * LANES, LANES)] = re * cos + im * sin
                                prep[rows, pl.ds((2 * kept + 1) * LANES, LANES)] = im * cos - re * sin
    z_done = three(dot, split(prep[...]), (z_in[0], z_in[1]))
    size = 8 * q_tiles
    parts = []
    for tile in range(4):
        rows = z_done[tile * size : (tile + 1) * size]
        column = lambda k: rows[:, k * LANES : (k + 1) * LANES]
        parts.append(
            (
                jnp.concatenate((column(0), column(2)), axis=0),
                jnp.concatenate((column(1), column(3)), axis=0),
            )
        )
    columns = []
    for j, (re, im) in enumerate(dft4(parts, -1.0)):
        if j:
            cos, sin = turns[0, :, j : j + 1], turns[0, :, 8 + j : 9 + j]
            re, im = re * cos + im * sin, im * cos - re * sin
        columns.append(jnp.concatenate((re, im), axis=0))
    ahead = three(dot, (y_in[0], y_in[1]), split(jnp.concatenate(columns, axis=1)))
    step = plan.major // 4
    scaled = []
    for j in range(4):
        own = ahead[:, j * LANES : (j + 1) * LANES]
        gain = jnp.concatenate([factor[pl.ds((j + 4 * m) * LANES, LANES), :] for m in range(step)], axis=0)
        scaled.append(own * jnp.concatenate((gain, gain), axis=0))
    back = three(dot, (y_out[0], y_out[1]), split(jnp.concatenate(scaled, axis=1)))
    parts = []
    for j in range(4):
        own = back[:, j * LANES : (j + 1) * LANES]
        re, im = own[: plan.quarter], own[plan.quarter :]
        if j:
            cos, sin = turns[1, :, j : j + 1], turns[1, :, 8 + j : 9 + j]
            re, im = re * cos - im * sin, im * cos + re * sin
        parts.append((re, im))
    lines = jnp.concatenate(
        [jnp.concatenate(part, axis=1) for part in dft4(parts, 1.0)], axis=0
    )
    done = three(dot, split(lines), (z_out[0], z_out[1]))
    cos, sin = lane_turn[4:5, :], lane_turn[5:6, :]
    re, im = done[:, :LANES], done[:, LANES:]
    out[:, 0] = (re * cos - im * sin).reshape(plan.n_col, LANES, LANES)
    out[:, 1] = (im * cos + re * sin).reshape(plan.n_col, LANES, LANES)


def middle(plan, got, factor, lane_turn, tables):
    return pl.pallas_call(
        functools.partial(middle_kernel, plan),
        out_shape=jax.ShapeDtypeStruct((plan.n_col, 2, LANES, LANES), F32),
        scratch_shapes=[
            pltpu.VMEM((8, 16, 8, LANES), F32),
            pltpu.VMEM((plan.grid // 2, 4 * LANES), F32),
        ],
        compiler_params=pltpu.CompilerParams(vmem_limit_bytes=VMEM_LIMIT),
        name="middle",
    )(got, factor, lane_turn, *tables)


def dft(parts, sign):
    size = len(parts)
    if size == 1:
        return parts
    even, odd = dft(parts[0::2], sign), dft(parts[1::2], sign)
    first, second = [], []
    for k in range(size // 2):
        (er, ei), (xr, xi) = even[k], odd[k]
        angle = 2 * math.pi * k / size
        if 4 * k == size:
            xr, xi = -sign * xi, sign * xr
        elif k:
            cos, sin = math.cos(angle), sign * math.sin(angle)
            xr, xi = xr * cos - xi * sin, xr * sin + xi * cos
        first.append((er + xr, ei + xi))
        second.append((er - xr, ei - xi))
    return first + second


def final_kernel(plan, got, *refs):
    out = refs[-1]
    scale = 1.0 / (plan.grid * plan.grid)
    step = 16

    @pl.loop(0, LANES // step)
    def _(i):
        rows = pl.ds(pl.multiple_of(i * step, step), step)
        parts = [(got[c, 0, rows, :], got[c, 1, rows, :]) for c in range(plan.n_col)]
        for w, (re, im) in enumerate(dft(parts, 1.0)):
            out[0, rows, pl.ds(w * LANES, LANES)] = re * scale
            out[1, rows, pl.ds(w * LANES, LANES)] = im * scale


def final(plan, pair, got, so_far):
    extra = [] if so_far is None else [so_far]
    shape = (plan.planes, LANES, plan.grid)
    return pl.pallas_call(
        functools.partial(final_kernel, plan),
        grid=(1,),
        in_specs=[pl.BlockSpec(got.shape, lambda i: (0, 0, 0, 0))]
        + [pl.BlockSpec(memory_space=pl.ANY) for _ in extra],
        out_specs=pl.BlockSpec((2, LANES, plan.grid), lambda i: (pair, 0, 0)),
        out_shape=jax.ShapeDtypeStruct(shape, F32),
        input_output_aliases={1: 0} if extra else {},
        compiler_params=pltpu.CompilerParams(vmem_limit_bytes=VMEM_LIMIT),
        name="final",
    )(got, *extra)


def lane_turns(plan):
    place, _ = plan.lane_z()
    low = np.stack((place, place + 64, np.arange(LANES))).astype(np.int32)
    phase = lax.axis_index("col") * jnp.asarray(low) % plan.grid
    angle = phase.astype(F32) * (2.0 * math.pi / plan.grid)
    both = jnp.stack((jnp.cos(angle), jnp.sin(angle)), axis=1).reshape(6, LANES)
    return jnp.concatenate((both, jnp.zeros((2, LANES), F32)), axis=0)


def body(n_row, n_col, top_coeffs, fresh_one, fresh_two, fresh_three, mixing, transfer):
    plan = Plan(n_row, n_col, top_coeffs.shape[1], transfer.shape[0])
    sends = expand(plan, top_coeffs, fresh_one, fresh_two, fresh_three, mixing)
    lane_turn = lane_turns(plan)
    y_in, y_out = plan.y_tables()
    tables = [
        jnp.asarray(t)
        for t in (halves(plan.z_table()), halves(y_in), halves(y_out), plan.turns(), halves(plan.z_back()))
    ]
    got = [
        lax.all_to_all(
            s.reshape(plan.owners, plan.src_rows, LANES), ("row", "col"), split_axis=0, concat_axis=0, tiled=True
        )
        for s in sends
    ]
    result = None
    for pair in range(plan.pairs):
        mid = middle(plan, got[pair], transfer, lane_turn, tables)
        back = lax.all_to_all(mid, "col", split_axis=0, concat_axis=0, tiled=True)
        result = final(plan, pair, back, result)
    return result


def solution(mesh):
    n_row, n_col = mesh.shape["row"], mesh.shape["col"]
    return jax.shard_map(
        functools.partial(body, n_row, n_col),
        mesh=mesh,
        in_specs=(
            P(None, ("row", "col")),
            P(None, ("row", "col")),
            P(None, None, ("row", "col")),
            P(None, None, ("row", "col")),
            P(),
            P(None, "col"),
        ),
        out_specs=P("row", "col", None),
        check_vma=False,
    )
```

```python
import functools
import math

import jax
import jax.numpy as jnp
import numpy as np
from jax import lax
from jax.experimental import pallas as pl
from jax.experimental.pallas import tpu as pltpu
from jax.sharding import PartitionSpec as P


F32 = jnp.float32
BF16 = jnp.bfloat16
LANES = 128
VMEM_LIMIT = 60 * 1024 * 1024


def bits_of(count):
    return count.bit_length() - 1


class Plan:
    def __init__(self, n_row, n_col, slots, grid):
        self.n_row, self.n_col, self.slots, self.grid = n_row, n_col, slots, grid
        self.owners = n_row * n_col
        self.planes = 16 // n_row
        self.pairs = self.planes // 2
        self.dest_x = n_row // 2
        self.blocks = grid // 8
        self.strip = self.blocks // n_col
        self.inner = slots // (2 * n_col)
        self.major = grid // LANES
        self.quarter = grid // 4
        own_bits = bits_of(self.owners)
        self.own_w = [k for k in range(own_bits) if k % 2 == 0]
        self.own_q = [k for k in range(own_bits) if k % 2 == 1]
        y_bits, z_bits = bits_of(self.strip), bits_of(self.blocks)
        code = []
        for k in range(y_bits):
            code += [("w", k), ("q", k)]
        code += [("w", k) for k in range(y_bits, z_bits)]
        self.inner_bits = code[own_bits:]
        top = bits_of(n_col)
        self.top_w = list(range(z_bits - top, z_bits))
        self.q_in = [k for kind, k in self.inner_bits if kind == "q"]
        self.mid_w = [k for kind, k in self.inner_bits if kind == "w" and k not in self.top_w]
        self.t_low = bits_of(LANES // self.inner)
        self.w_kept = 2 ** len(self.mid_w)
        self.rows_rw = 2 * self.w_kept
        self.small = 2 ** (self.t_low + len(self.q_in))
        assert self.small == 8 and n_col == self.major and slots // 2 == 4 * LANES
        self.src_rows = self.rows_rw * 2 * self.small
        self.q_stack = LANES // self.src_rows
        self.q_rest = 2 ** len(self.own_q) // self.q_stack
        self.w_extra = 2 ** len(self.own_w) // 8
        assert self.w_extra * self.w_kept == 2
        assert self.pairs in (1, 2)

    def send_table(self):
        lane = np.arange(LANES)
        low_t, inner = lane // self.inner, lane % self.inner
        top = np.zeros(LANES, np.int64)
        small = low_t.copy()
        kept = np.zeros(LANES, np.int64)
        q_value = np.zeros(LANES, np.int64)
        for place, (kind, k) in enumerate(self.inner_bits):
            bit = (inner >> place) & 1
            if kind == "q":
                q_value += bit << self.q_in.index(k)
            elif k in self.top_w:
                top += bit << self.top_w.index(k)
            else:
                kept += bit << self.mid_w.index(k)
        small = (low_t << len(self.q_in)) + q_value
        table = np.zeros((self.n_col, 2, self.w_kept, self.small, 2, LANES))
        for c in range(self.n_col):
            angle = 2 * np.pi * (c * top % self.n_col) / self.n_col
            cos, sin = np.cos(angle), np.sin(angle)
            table[c, 0, kept, small, 0, lane] = cos
            table[c, 0, kept, small, 1, lane] = sin
            table[c, 1, kept, small, 0, lane] = -sin
            table[c, 1, kept, small, 1, lane] = cos
        return table.reshape(self.n_col * self.rows_rw * self.small, 2 * LANES)

    def lane_z(self):
        lane = np.arange(LANES)
        return (lane >> 4) * 8 + ((lane >> 3) & 1) * 4 + (lane & 3), (lane >> 2) & 1

    def z_table(self):
        low, y_bit = self.lane_z()
        k = np.arange(LANES)
        table = np.zeros((2, 2, LANES, 2, 2, LANES))
        for kept in range(2):
            phase = np.outer(64 * kept + low, k) % LANES
            cos, sin = np.cos(2 * np.pi * phase / LANES), np.sin(2 * np.pi * phase / LANES)
            for b in range(2):
                mask = (y_bit == b)[:, None]
                table[kept, 0, :, b, 0] = cos * mask
                table[kept, 1, :, b, 0] = sin * mask
                table[kept, 0, :, b, 1] = -sin * mask
                table[kept, 1, :, b, 1] = cos * mask
        return table.reshape(4 * LANES, 4 * LANES)

    def y_rows(self):
        shape = (2, self.q_rest, 4, self.q_stack, self.small)
        y0, q_rest, y21, q_stack, small = np.indices(shape)
        n_in = len(self.q_in)
        t_low, q_in = small >> n_in, small & (2 ** n_in - 1)
        q_local = q_in * 2 ** len(self.own_q) + q_rest * self.q_stack + q_stack
        return (t_low * LANES + q_local * 8 + y21 * 2 + y0).reshape(-1)

    def m_rows(self):
        step = self.major // 4
        return (np.arange(step)[:, None] + step * np.arange(LANES)[None, :]).reshape(-1)

    def y_tables(self):
        n2, m, size = self.y_rows(), self.m_rows(), self.quarter
        angle = 2 * np.pi * (np.outer(m, n2) % size) / size
        cos, sin = np.cos(angle), np.sin(angle)
        ahead = np.block([[cos, sin], [-sin, cos]])
        angle = 2 * np.pi * (np.outer(np.arange(size), m) % size) / size
        cos, sin = np.cos(angle), np.sin(angle)
        return ahead, np.block([[cos, -sin], [sin, cos]])

    def turns(self):
        out = np.zeros((2, self.quarter, LANES), np.float32)
        for order, n2 in enumerate((self.y_rows(), np.arange(self.quarter))):
            for j in range(4):
                angle = 2 * np.pi * (n2 * j) / self.grid
                out[order, :, j] = np.cos(angle)
                out[order, :, 8 + j] = np.sin(angle)
        return out

    def z_back(self):
        n = np.arange(LANES)
        angle = 2 * np.pi * (np.outer(n, n) % LANES) / LANES
        cos, sin = np.cos(angle), np.sin(angle)
        return np.block([[cos, sin], [-sin, cos]])

    def src(self, w, q):
        index = 0
        for place, bit in enumerate(self.own_w):
            index |= ((w >> place) & 1) << bit
        for place, bit in enumerate(self.own_q):
            index |= ((q >> place) & 1) << bit
        return index


def halves(table):
    high = np.asarray(table, np.float32).astype(BF16)
    low = (np.asarray(table, np.float64) - high.astype(np.float64)).astype(BF16)
    return np.stack((high, low))


def split(x):
    high = x.astype(BF16)
    return high, (x - high.astype(F32)).astype(BF16)


def dot(a, b):
    return jnp.dot(a, b, preferred_element_type=F32)


def dot_nt(a, b):
    return lax.dot_general(a, b, (((1,), (1,)), ((), ())), preferred_element_type=F32)


def three(f, a, b):
    return f(a[0], b[0]) + (f(a[0], b[1]) + f(a[1], b[0]))


def one_hot(shape, hit):
    row = lax.broadcasted_iota(jnp.int32, shape, 0)
    col = lax.broadcasted_iota(jnp.int32, shape, 1)
    return jnp.where(hit(row, col), 1.0, 0.0).astype(BF16)


def spread(mixing, rows, row_of, same, fresh):
    pick = one_hot((rows, 64), lambda r, c: c == row_of(r))
    if fresh:
        wide = one_hot((64, 448), lambda r, c: r == 8 + c // 8)
        cell = lambda c: c % 8
    else:
        wide = one_hot((64, 64), lambda r, c: r == c % 8)
        cell = lambda c: c // 8
    table = dot(dot(pick, mixing).astype(BF16), wide)
    row = lax.broadcasted_iota(jnp.int32, table.shape, 0)
    col = lax.broadcasted_iota(jnp.int32, table.shape, 1)
    return jnp.where(same(row) == cell(col), table, 0.0).astype(BF16)


def carry(table, parents):
    high = parents.astype(BF16)
    rest = parents - high.astype(F32)
    mid = rest.astype(BF16)
    low = (rest - mid.astype(F32)).astype(BF16)
    return dot(table, high) + (dot(table, mid) + dot(table, low))


def expand_kernel(plan, top, one, two, three_ref, mixing, send, *refs):
    count = plan.pairs if plan.pairs == 1 else plan.n_row + 1
    outs = refs[:count]
    leaf, w2f, w2p, w3f, w3p, joined = refs[count:]
    step = pl.program_id(0)

    @pl.when(step == 0)
    def _():
        mix = mixing[...]
        w2f[...] = spread(mix, 512, lambda r: r % 64, lambda r: r // 64, True)
        w2p[...] = spread(mix, 512, lambda r: r % 64, lambda r: r // 64, False)
        child = lambda r: 8 * (4 * (r // 32 % 2) + 2 * (r // 4 % 2) + r % 2)
        cell = lambda r: 4 * (r // 16 % 2) + 2 * (r // 8 % 2) + r // 2 % 2
        w3f[...] = spread(mix, 64, child, cell, True)
        w3p[...] = spread(mix, 64, child, cell, False)

    mix = mixing[...]
    level = carry(mix[:, :8], top[...]) + dot(mix[:, 8:], one[...])
    for g in range(8):
        rows = pl.ds(64 * g, 64)
        second = dot(w2f[rows, :], two[...]) + carry(w2p[rows, :], level)
        fresh = three_ref[:, pl.ds(8 * g, 8), :].reshape(448, second.shape[1])
        leaf[g] = dot(w3f[...], fresh) + carry(w3p[...], second)
    table = (send[0], send[1])
    for x in range(4):
        x2, x1 = x // 2, x % 2
        pair, dest = x % plan.pairs, x // plan.pairs
        for high in range(2):
            parts = []
            for part in range(2):
                pieces = [
                    leaf[4 * x2 + yz, pl.ds(32 * part + 16 * x1, 16), pl.ds((2 * high + tau) * LANES, LANES)]
                    for tau in range(2)
                    for yz in range(4)
                ]
                parts.append(jnp.concatenate(pieces, axis=0))
            data = split(jnp.concatenate(parts, axis=1))
            sent = three(dot_nt, table, data)
            sent = sent.reshape(plan.n_col, plan.rows_rw, plan.small, LANES)
            if pair == 0:
                outs[0][0, dest, :, :, high] = sent
            else:
                joined[step * plan.dest_x + dest, :, :, high] = sent

    if plan.pairs > 1:

        @pl.when(step == 1)
        def _():
            row, col = lax.axis_index("row"), lax.axis_index("col")
            for far in range(plan.n_row):
                for shift in range(plan.n_col):
                    outs[1 + far][shift] = joined[row ^ far, col ^ shift]


def expand(plan, top, one, two, three_in, mixing):
    half = plan.slots // 2
    block = (plan.n_col, plan.rows_rw, 2, plan.small, LANES)
    shapes = [(2, plan.dest_x) + block]
    specs = [pl.BlockSpec((1, plan.dest_x) + block, lambda i: (i, 0, 0, 0, 0, 0, 0))]
    if plan.pairs > 1:
        shapes += [block] * plan.n_row
        specs += [pl.BlockSpec(block, lambda i: (0, 0, 0, 0, 0))] * plan.n_row
    table = halves(plan.send_table())
    whole = lambda array: pl.BlockSpec(array.shape, lambda i: (0,) * array.ndim)
    return pl.pallas_call(
        functools.partial(expand_kernel, plan),
        grid=(2,),
        in_specs=[
            pl.BlockSpec((8, half), lambda i: (0, i)),
            pl.BlockSpec((56, half), lambda i: (0, i)),
            pl.BlockSpec((448, half), lambda i: (0, i)),
            pl.BlockSpec((56, 64, half), lambda i: (0, 0, i)),
            whole(mixing),
            whole(table),
        ],
        out_specs=specs,
        out_shape=[jax.ShapeDtypeStruct(shape, F32) for shape in shapes],
        scratch_shapes=[
            pltpu.VMEM((8, 64, half), F32),
            pltpu.VMEM((512, 448), BF16),
            pltpu.VMEM((512, 64), BF16),
            pltpu.VMEM((64, 448), BF16),
            pltpu.VMEM((64, 64), BF16),
            pltpu.VMEM((plan.n_row,) + block, F32),
        ],
        compiler_params=pltpu.CompilerParams(vmem_limit_bytes=VMEM_LIMIT),
        name="expand",
    )(top, one, two.reshape(448, plan.slots), three_in, mixing, jnp.asarray(table))


def dft4(parts, sign):
    (ar, ai), (br, bi), (cr, ci), (dr, di) = parts
    pr, pi, mr, mi = ar + cr, ai + ci, ar - cr, ai - ci
    qr, qi, nr, ni = br + dr, bi + di, br - dr, bi - di
    return [
        (pr + qr, pi + qi),
        (mr - sign * ni, mi + sign * nr),
        (pr - qr, pi - qi),
        (mr + sign * ni, mi - sign * nr),
    ]


def middle_kernel(plan, count, *refs):
    parts, refs = refs[:count], refs[count:]
    factor, lane_turn, z_in, y_in, y_out, turns, z_out = refs[:7]
    outs = refs[7 : 7 + plan.n_col]
    got, flipped, prep, out = refs[7 + plan.n_col :]
    row, col = lax.axis_index("row"), lax.axis_index("col")
    if count == 1:
        got = parts[0]
    else:
        for shift in range(plan.n_col):
            for far in range(plan.n_row):
                got[(row ^ far) * plan.n_col + (col ^ shift)] = parts[shift][far]
    q_tiles = plan.q_rest * 4 * plan.q_stack
    for q_rest in range(plan.q_rest):
        for extra in range(plan.w_extra):
            for w in range(8):
                stack = [
                    got[plan.src(extra * 8 + w, q_rest * plan.q_stack + q)]
                    for q in range(plan.q_stack)
                ]
                flipped[w] = jnp.concatenate(stack, axis=0).T.reshape(16, 8, LANES)
            for tau in range(2):
                for y21 in range(4):
                    y2, y1 = y21 // 2, y21 % 2
                    pieces = [
                        flipped[w, 8 * tau + 4 * y2 + 2 * z2 + y1] for w in range(8) for z2 in range(2)
                    ]
                    block = jnp.concatenate(pieces, axis=0).T
                    block = block.reshape(plan.q_stack, 2, plan.w_kept, 2, 8, LANES)
                    for kept_in in range(plan.w_kept):
                        kept = extra if plan.w_extra == 2 else kept_in
                        cos = lane_turn[2 * kept : 2 * kept + 1, :]
                        sin = lane_turn[2 * kept + 1 : 2 * kept + 2, :]
                        for q in range(plan.q_stack):
                            for high in range(2):
                                re, im = block[q, 0, kept_in, high], block[q, 1, kept_in, high]
                                tile = (2 * high + tau) * q_tiles + (q_rest * 4 + y21) * plan.q_stack + q
                                rows = pl.ds(8 * tile, 8)
                                prep[rows, pl.ds(2 * kept * LANES, LANES)] = re * cos + im * sin
                                prep[rows, pl.ds((2 * kept + 1) * LANES, LANES)] = im * cos - re * sin
    z_done = three(dot, split(prep[...]), (z_in[0], z_in[1]))
    size = 8 * q_tiles
    parts = []
    for tile in range(4):
        rows = z_done[tile * size : (tile + 1) * size]
        column = lambda k: rows[:, k * LANES : (k + 1) * LANES]
        parts.append(
            (
                jnp.concatenate((column(0), column(2)), axis=0),
                jnp.concatenate((column(1), column(3)), axis=0),
            )
        )
    columns = []
    for j, (re, im) in enumerate(dft4(parts, -1.0)):
        if j:
            cos, sin = turns[0, :, j : j + 1], turns[0, :, 8 + j : 9 + j]
            re, im = re * cos + im * sin, im * cos - re * sin
        columns.append(jnp.concatenate((re, im), axis=0))
    ahead = three(dot, (y_in[0], y_in[1]), split(jnp.concatenate(columns, axis=1)))
    step = plan.major // 4
    scaled = []
    for j in range(4):
        own = ahead[:, j * LANES : (j + 1) * LANES]
        gain = jnp.concatenate([factor[pl.ds((j + 4 * m) * LANES, LANES), :] for m in range(step)], axis=0)
        scaled.append(own * jnp.concatenate((gain, gain), axis=0))
    back = three(dot, (y_out[0], y_out[1]), split(jnp.concatenate(scaled, axis=1)))
    parts = []
    for j in range(4):
        own = back[:, j * LANES : (j + 1) * LANES]
        re, im = own[: plan.quarter], own[plan.quarter :]
        if j:
            cos, sin = turns[1, :, j : j + 1], turns[1, :, 8 + j : 9 + j]
            re, im = re * cos - im * sin, im * cos + re * sin
        parts.append((re, im))
    lines = jnp.concatenate(
        [jnp.concatenate(part, axis=1) for part in dft4(parts, 1.0)], axis=0
    )
    done = three(dot, split(lines), (z_out[0], z_out[1]))
    cos, sin = lane_turn[4:5, :], lane_turn[5:6, :]
    re, im = done[:, :LANES], done[:, LANES:]
    out[:, 0] = (re * cos - im * sin).reshape(plan.n_col, LANES, LANES)
    out[:, 1] = (im * cos + re * sin).reshape(plan.n_col, LANES, LANES)
    for shift in range(plan.n_col):
        outs[shift][...] = out[col ^ shift]


def middle(plan, parts, factor, lane_turn, tables):
    return pl.pallas_call(
        functools.partial(middle_kernel, plan, len(parts)),
        out_shape=[jax.ShapeDtypeStruct((2, LANES, LANES), F32)] * plan.n_col,
        scratch_shapes=[
            pltpu.VMEM((plan.owners, plan.src_rows, LANES), F32),
            pltpu.VMEM((8, 16, 8, LANES), F32),
            pltpu.VMEM((plan.grid // 2, 4 * LANES), F32),
            pltpu.VMEM((plan.n_col, 2, LANES, LANES), F32),
        ],
        compiler_params=pltpu.CompilerParams(vmem_limit_bytes=VMEM_LIMIT),
        name="middle",
    )(*parts, factor, lane_turn, *tables)


def regroup_kernel(plan, *refs):
    parts, outs = refs[: plan.n_row], refs[plan.n_row :]
    for shift in range(plan.n_col):
        for far in range(plan.n_row):
            outs[shift][far] = parts[far][shift]


def regroup(plan, parts):
    return pl.pallas_call(
        functools.partial(regroup_kernel, plan),
        out_shape=[jax.ShapeDtypeStruct((plan.n_row, plan.src_rows, LANES), F32)] * plan.n_col,
        compiler_params=pltpu.CompilerParams(vmem_limit_bytes=VMEM_LIMIT),
        name="regroup",
    )(*parts)


def swap(parts, axis):
    size = len(parts)
    out = [parts[0]] + [None] * (size - 1)
    for shift in reversed(range(1, size)):
        out[shift] = lax.ppermute(parts[shift], axis, [(k, k ^ shift) for k in range(size)])
    return out


def dft(parts, sign):
    size = len(parts)
    if size == 1:
        return parts
    even, odd = dft(parts[0::2], sign), dft(parts[1::2], sign)
    first, second = [], []
    for k in range(size // 2):
        (er, ei), (xr, xi) = even[k], odd[k]
        angle = 2 * math.pi * k / size
        if 4 * k == size:
            xr, xi = -sign * xi, sign * xr
        elif k:
            cos, sin = math.cos(angle), sign * math.sin(angle)
            xr, xi = xr * cos - xi * sin, xr * sin + xi * cos
        first.append((er + xr, ei + xi))
        second.append((er - xr, ei - xi))
    return first + second


def final_kernel(plan, *refs):
    parts, out, got = refs[: plan.n_col], refs[-2], refs[-1]
    scale = 1.0 / (plan.grid * plan.grid)
    step = 16
    col = lax.axis_index("col")
    for shift in range(plan.n_col):
        got[col ^ shift] = parts[shift][...]

    @pl.loop(0, LANES // step)
    def _(i):
        rows = pl.ds(pl.multiple_of(i * step, step), step)
        parts = [(got[c, 0, rows, :], got[c, 1, rows, :]) for c in range(plan.n_col)]
        for w, (re, im) in enumerate(dft(parts, 1.0)):
            out[0, rows, pl.ds(w * LANES, LANES)] = re * scale
            out[1, rows, pl.ds(w * LANES, LANES)] = im * scale


def final(plan, pair, parts, so_far):
    extra = [] if so_far is None else [so_far]
    shape = (plan.planes, LANES, plan.grid)
    return pl.pallas_call(
        functools.partial(final_kernel, plan),
        grid=(1,),
        in_specs=[pl.BlockSpec((2, LANES, LANES), lambda i: (0, 0, 0))] * plan.n_col
        + [pl.BlockSpec(memory_space=pl.ANY) for _ in extra],
        out_specs=pl.BlockSpec((2, LANES, plan.grid), lambda i: (pair, 0, 0)),
        out_shape=jax.ShapeDtypeStruct(shape, F32),
        scratch_shapes=[pltpu.VMEM((plan.n_col, 2, LANES, LANES), F32)],
        input_output_aliases={plan.n_col: 0} if extra else {},
        compiler_params=pltpu.CompilerParams(vmem_limit_bytes=VMEM_LIMIT),
        name="final",
    )(*parts, *extra)


def lane_turns(plan):
    place, _ = plan.lane_z()
    low = np.stack((place, place + 64, np.arange(LANES))).astype(np.int32)
    phase = lax.axis_index("col") * jnp.asarray(low) % plan.grid
    angle = phase.astype(F32) * (2.0 * math.pi / plan.grid)
    both = jnp.stack((jnp.cos(angle), jnp.sin(angle)), axis=1).reshape(6, LANES)
    return jnp.concatenate((both, jnp.zeros((2, LANES), F32)), axis=0)


def steps(n_row, n_col, top_coeffs, fresh_one, fresh_two, fresh_three, mixing, transfer):
    plan = Plan(n_row, n_col, top_coeffs.shape[1], transfer.shape[0])
    sends = list(expand(plan, top_coeffs, fresh_one, fresh_two, fresh_three, mixing))
    lane_turn = lane_turns(plan)
    y_in, y_out = plan.y_tables()
    tables = [
        jnp.asarray(t)
        for t in (halves(plan.z_table()), halves(y_in), halves(y_out), plan.turns(), halves(plan.z_back()))
    ]
    got = []
    sent = sends[0].reshape(plan.owners, plan.src_rows, LANES)
    got.append([lax.all_to_all(sent, ("row", "col"), split_axis=0, concat_axis=0, tiled=True)])
    if plan.pairs > 1:
        rows = swap([s.reshape(plan.n_col, plan.src_rows, LANES) for s in sends[1:]], "row")
        columns = regroup(plan, rows)
        got.append(swap(columns, "col"))
    result = None
    for pair in range(plan.pairs):
        mid = middle(plan, got[pair], transfer, lane_turn, tables)
        back = swap(mid, "col")
        result = final(plan, pair, back, result)
    return result


def solution(mesh):
    n_row, n_col = mesh.shape["row"], mesh.shape["col"]
    return jax.shard_map(
        functools.partial(steps, n_row, n_col),
        mesh=mesh,
        in_specs=(
            P(None, ("row", "col")),
            P(None, ("row", "col")),
            P(None, None, ("row", "col")),
            P(None, None, ("row", "col")),
            P(),
            P(None, "col"),
        ),
        out_specs=P("row", "col", None),
        check_vma=False,
    )
```

```python
import functools
import math

import jax
import jax.numpy as jnp
import numpy as np
from jax import lax
from jax.experimental import pallas as pl
from jax.experimental.pallas import tpu as pltpu
from jax.sharding import PartitionSpec as P


F32 = jnp.float32
BF16 = jnp.bfloat16
LANES = 128
VMEM_LIMIT = 60 * 1024 * 1024


def bits_of(count):
    return count.bit_length() - 1


class Plan:
    def __init__(self, n_row, n_col, slots, grid):
        self.n_row, self.n_col, self.slots, self.grid = n_row, n_col, slots, grid
        self.owners = n_row * n_col
        self.planes = 16 // n_row
        self.pairs = self.planes // 2
        self.dest_x = n_row // 2
        self.blocks = grid // 8
        self.strip = self.blocks // n_col
        self.inner = slots // (2 * n_col)
        self.major = grid // LANES
        self.quarter = grid // 4
        own_bits = bits_of(self.owners)
        self.own_w = [k for k in range(own_bits) if k % 2 == 0]
        self.own_q = [k for k in range(own_bits) if k % 2 == 1]
        y_bits, z_bits = bits_of(self.strip), bits_of(self.blocks)
        code = []
        for k in range(y_bits):
            code += [("w", k), ("q", k)]
        code += [("w", k) for k in range(y_bits, z_bits)]
        self.inner_bits = code[own_bits:]
        top = bits_of(n_col)
        self.top_w = list(range(z_bits - top, z_bits))
        self.q_in = [k for kind, k in self.inner_bits if kind == "q"]
        self.mid_w = [k for kind, k in self.inner_bits if kind == "w" and k not in self.top_w]
        self.t_low = bits_of(LANES // self.inner)
        self.w_kept = 2 ** len(self.mid_w)
        self.rows_rw = 2 * self.w_kept
        self.small = 2 ** (self.t_low + len(self.q_in))
        assert self.small == 8 and n_col == self.major and slots // 2 == 4 * LANES
        self.src_rows = self.rows_rw * 2 * self.small
        self.group = self.rows_rw * self.small
        self.spare = LANES // self.group // 4
        self.own_qs = 2 ** len(self.own_q)
        self.w_extra = 2 ** len(self.own_w) // 8
        assert self.w_extra * self.w_kept == 2
        assert self.pairs in (1, 2)

    def send_table(self):
        lane = np.arange(LANES)
        low_t, inner = lane // self.inner, lane % self.inner
        top = np.zeros(LANES, np.int64)
        small = low_t.copy()
        kept = np.zeros(LANES, np.int64)
        q_value = np.zeros(LANES, np.int64)
        for place, (kind, k) in enumerate(self.inner_bits):
            bit = (inner >> place) & 1
            if kind == "q":
                q_value += bit << self.q_in.index(k)
            elif k in self.top_w:
                top += bit << self.top_w.index(k)
            else:
                kept += bit << self.mid_w.index(k)
        small = (low_t << len(self.q_in)) + q_value
        table = np.zeros((self.n_col, 2, self.w_kept, self.small, 2, LANES))
        for c in range(self.n_col):
            angle = 2 * np.pi * (c * top % self.n_col) / self.n_col
            cos, sin = np.cos(angle), np.sin(angle)
            table[c, 0, kept, small, 0, lane] = cos
            table[c, 0, kept, small, 1, lane] = sin
            table[c, 1, kept, small, 0, lane] = -sin
            table[c, 1, kept, small, 1, lane] = cos
        return table.reshape(self.n_col * self.rows_rw * self.small, 2 * LANES)

    def lane_z(self):
        lane = np.arange(LANES)
        return (lane >> 4) * 8 + ((lane >> 3) & 1) * 4 + (lane & 3), (lane >> 2) & 1

    def z_table(self):
        low, y_bit = self.lane_z()
        k = np.arange(LANES)
        table = np.zeros((2, 2, LANES, 2, 2, LANES))
        for kept in range(2):
            phase = np.outer(64 * kept + low, k) % LANES
            cos, sin = np.cos(2 * np.pi * phase / LANES), np.sin(2 * np.pi * phase / LANES)
            for b in range(2):
                mask = (y_bit == b)[:, None]
                table[kept, 0, :, b, 0] = cos * mask
                table[kept, 1, :, b, 0] = sin * mask
                table[kept, 0, :, b, 1] = -sin * mask
                table[kept, 1, :, b, 1] = cos * mask
        return table.reshape(4 * LANES, 4 * LANES)

    def y_rows(self):
        y0, own, y21, small = np.indices((2, self.own_qs, 4, self.small))
        n_in = len(self.q_in)
        t_low, q_in = small >> n_in, small & (2 ** n_in - 1)
        q_local = q_in * self.own_qs + own
        return (t_low * LANES + q_local * 8 + y21 * 2 + y0).reshape(-1)

    def m_rows(self):
        step = self.major // 4
        return (np.arange(step)[:, None] + step * np.arange(LANES)[None, :]).reshape(-1)

    def y_tables(self):
        n2, m, size = self.y_rows(), self.m_rows(), self.quarter
        angle = 2 * np.pi * (np.outer(m, n2) % size) / size
        cos, sin = np.cos(angle), np.sin(angle)
        ahead = np.block([[cos, sin], [-sin, cos]])
        angle = 2 * np.pi * (np.outer(np.arange(size), m) % size) / size
        cos, sin = np.cos(angle), np.sin(angle)
        return ahead, np.block([[cos, -sin], [sin, cos]])

    def turns(self):
        out = np.zeros((2, self.quarter, LANES), np.float32)
        for order, n2 in enumerate((self.y_rows(), np.arange(self.quarter))):
            for j in range(4):
                angle = 2 * np.pi * (n2 * j) / self.grid
                out[order, :, j] = np.cos(angle)
                out[order, :, 8 + j] = np.sin(angle)
        return out

    def z_back(self):
        n = np.arange(LANES)
        angle = 2 * np.pi * (np.outer(n, n) % LANES) / LANES
        cos, sin = np.cos(angle), np.sin(angle)
        return np.block([[cos, sin], [-sin, cos]])

    def src(self, w, q):
        index = 0
        for place, bit in enumerate(self.own_w):
            index |= ((w >> place) & 1) << bit
        for place, bit in enumerate(self.own_q):
            index |= ((q >> place) & 1) << bit
        return index


def halves(table):
    high = np.asarray(table, np.float32).astype(BF16)
    low = (np.asarray(table, np.float64) - high.astype(np.float64)).astype(BF16)
    return np.stack((high, low))


def split(x):
    high = x.astype(BF16)
    return high, (x - high.astype(F32)).astype(BF16)


def dot(a, b):
    return jnp.dot(a, b, preferred_element_type=F32)


def three(f, a, b):
    return f(a[0], b[0]) + (f(a[0], b[1]) + f(a[1], b[0]))


def one_hot(shape, hit):
    row = lax.broadcasted_iota(jnp.int32, shape, 0)
    col = lax.broadcasted_iota(jnp.int32, shape, 1)
    return jnp.where(hit(row, col), 1.0, 0.0).astype(BF16)


def spread(table, rows, row_of, same):
    pick = one_hot((rows, 64), lambda r, c: c == row_of(r))
    wide = one_hot((64, 448), lambda r, c: r == 8 + c // 8)
    table = dot(dot(pick, table).astype(BF16), wide)
    row = lax.broadcasted_iota(jnp.int32, table.shape, 0)
    col = lax.broadcasted_iota(jnp.int32, table.shape, 1)
    return jnp.where(same(row) == col % 8, table, 0.0).astype(BF16)


def lane_groups(arrays, group):
    lane = lax.broadcasted_iota(jnp.int32, arrays[0].shape, 1) // group
    arrays, step = list(arrays), 1
    while step < len(arrays):
        low = (lane // step) % 2 == 0
        for k in range(len(arrays)):
            if k // step % 2 == 0:
                a, b = arrays[k], arrays[k + step]
                arrays[k] = jnp.where(low, a, pltpu.roll(b, group * step, 1))
                arrays[k + step] = jnp.where(low, pltpu.roll(a, LANES - group * step, 1), b)
        step *= 2
    return arrays


def expand_kernel(plan, top, one, two, three_ref, mixing, send, *refs):
    count = plan.pairs if plan.pairs == 1 else plan.n_row + 1
    outs = refs[:count]
    leaf, w_one, w_two, w_three, joined = refs[count:]
    step = pl.program_id(0)

    @pl.when(step == 0)
    def _():
        mix = mixing[...]
        child = lambda r: 8 * (4 * (r // 32 % 2) + 2 * (r // 4 % 2) + r % 2)
        cell = lambda r: 4 * (r // 16 % 2) + 2 * (r // 8 % 2) + r // 2 % 2
        w_three[...] = spread(mix, 64, child, cell)
        last = dot(dot(one_hot((64, 64), lambda r, c: c == child(r)), mix).astype(BF16), one_hot((64, 64), lambda r, c: r == c % 8))
        row = lax.broadcasted_iota(jnp.int32, (64, 64), 0)
        col = lax.broadcasted_iota(jnp.int32, (64, 64), 1)
        through = dot(jnp.where(cell(row) == col // 8, last, 0.0).astype(BF16), mix)
        parts = split(through)
        for k in range(2):
            w_two[pl.ds(512 * k, 512), :] = spread(parts[k], 512, lambda r: r % 64, lambda r: r // 64)
        for c in range(8):
            own = mix[8 * c : 8 * c + 8, :]
            table = split(dot(parts[0][:, :8], own) + dot(parts[1][:, :8], own))
            for k in range(2):
                w_one[pl.ds(64 * c, 64), pl.ds(64 * k, 64)] = table[k]

    upper, lower = split(top[...])
    ones = jnp.concatenate((upper, one[...]), axis=0)
    blocks = jnp.concatenate((ones, ones), axis=0)
    twos = dot(w_two[...], two[...])
    second = twos[:512] + (twos[512:] + (dot(w_one[...], blocks) + dot(w_one[:, :8], lower)))
    for g in range(8):
        fresh = three_ref[:, pl.ds(8 * g, 8), :].reshape(448, second.shape[1])
        leaf[g] = dot(w_three[...], fresh) + second[64 * g : 64 * g + 64]
    table = (send[0], send[1])
    for x in range(4):
        x2, x1 = x // 2, x % 2
        pair, dest = x % plan.pairs, x // plan.pairs
        parts = []
        for part in range(2):
            pieces = [
                leaf[4 * x2 + yz, pl.ds(32 * part + 16 * x1, 16), pl.ds(tile * LANES, LANES)]
                for tile in range(4)
                for yz in range(4)
            ]
            parts.append(jnp.concatenate(pieces, axis=0))
        sent = three(dot, split(jnp.concatenate(parts, axis=1)), table)
        for side in range(2):
            pieces = []
            for spare in range(plan.spare):
                for tau in range(2):
                    for high in range(2):
                        start = (2 * high + tau) * 64 + spare * plan.src_rows
                        pieces.append(
                            sent[start : start + plan.src_rows, side * LANES : (side + 1) * LANES]
                        )
            for k, piece in enumerate(lane_groups(pieces, plan.group)):
                c = side * (plan.n_col // 2) + k
                if pair == 0:
                    outs[0][0, dest, c] = piece
                else:
                    joined[step * plan.dest_x + dest, c] = piece

    if plan.pairs > 1:

        @pl.when(step == 1)
        def _():
            row, col = lax.axis_index("row"), lax.axis_index("col")
            for far in range(plan.n_row):
                for shift in range(plan.n_col):
                    outs[1 + far][shift] = joined[row ^ far, col ^ shift]


def expand(plan, top, one, two, three_in, mixing):
    lanes = plan.slots // 2
    block = (plan.n_col, plan.src_rows, LANES)
    shapes = [(2, plan.dest_x) + block]
    specs = [pl.BlockSpec((1, plan.dest_x) + block, lambda i: (i, 0, 0, 0, 0))]
    if plan.pairs > 1:
        shapes += [block] * plan.n_row
        specs += [pl.BlockSpec(block, lambda i: (0, 0, 0))] * plan.n_row
    table = halves(plan.send_table().T)
    whole = lambda array: pl.BlockSpec(array.shape, lambda i: (0,) * array.ndim)
    return pl.pallas_call(
        functools.partial(expand_kernel, plan),
        grid=(2,),
        in_specs=[
            pl.BlockSpec((8, lanes), lambda i: (0, i)),
            pl.BlockSpec((56, lanes), lambda i: (0, i)),
            pl.BlockSpec((448, lanes), lambda i: (0, i)),
            pl.BlockSpec((56, 64, lanes), lambda i: (0, 0, i)),
            whole(mixing),
            whole(table),
        ],
        out_specs=specs,
        out_shape=[jax.ShapeDtypeStruct(shape, F32) for shape in shapes],
        scratch_shapes=[
            pltpu.VMEM((8, 64, lanes), F32),
            pltpu.VMEM((512, 128), BF16),
            pltpu.VMEM((1024, 448), BF16),
            pltpu.VMEM((64, 448), BF16),
            pltpu.VMEM((plan.n_row,) + block, F32),
        ],
        compiler_params=pltpu.CompilerParams(vmem_limit_bytes=VMEM_LIMIT),
        name="expand",
    )(top, one, two.reshape(448, plan.slots), three_in, mixing, jnp.asarray(table))


def dft4(parts, sign):
    (ar, ai), (br, bi), (cr, ci), (dr, di) = parts
    pr, pi, mr, mi = ar + cr, ai + ci, ar - cr, ai - ci
    qr, qi, nr, ni = br + dr, bi + di, br - dr, bi - di
    return [
        (pr + qr, pi + qi),
        (mr - sign * ni, mi + sign * nr),
        (pr - qr, pi - qi),
        (mr + sign * ni, mi - sign * nr),
    ]


def middle_kernel(plan, count, *refs):
    parts, refs = refs[:count], refs[count:]
    factor, lane_turn, z_in, y_in, y_out, turns, z_out = refs[:7]
    outs = refs[7 : 7 + plan.n_col]
    got, prep, out = refs[7 + plan.n_col :]
    row, col = lax.axis_index("row"), lax.axis_index("col")
    if count == 1:
        got = parts[0]
    else:
        for shift in range(plan.n_col):
            for far in range(plan.n_row):
                got[(row ^ far) * plan.n_col + (col ^ shift)] = parts[shift][far]
    q_tiles = plan.own_qs * 4
    for q in range(plan.own_qs):
        for extra in range(plan.w_extra):
            for y21 in range(4 // plan.spare):
                y2, y1 = y21 // 2, y21 % 2
                pieces = [
                    got[plan.src(extra * 8 + w, q), pl.ds(8 * (4 * y2 + 2 * z2 + y1), 8), :]
                    for w in range(8)
                    for z2 in range(2)
                ]
                block = jnp.concatenate(pieces, axis=0).T
                block = block.reshape(plan.spare, 2, 2, 2, plan.w_kept, 8, LANES)
                for kept_in in range(plan.w_kept):
                    kept = extra if plan.w_extra == 2 else kept_in
                    cos = lane_turn[2 * kept : 2 * kept + 1, :]
                    sin = lane_turn[2 * kept + 1 : 2 * kept + 2, :]
                    for spare in range(plan.spare):
                        for tau in range(2):
                            for high in range(2):
                                re = block[spare, tau, high, 0, kept_in]
                                im = block[spare, tau, high, 1, kept_in]
                                tile = (2 * high + tau) * q_tiles + q * 4 + spare * 2 + y21
                                rows = pl.ds(8 * tile, 8)
                                prep[rows, pl.ds(2 * kept * LANES, LANES)] = re * cos + im * sin
                                prep[rows, pl.ds((2 * kept + 1) * LANES, LANES)] = im * cos - re * sin
    z_done = three(dot, split(prep[...]), (z_in[0], z_in[1]))
    size = 8 * q_tiles
    parts = []
    for tile in range(4):
        rows = z_done[tile * size : (tile + 1) * size]
        column = lambda k: rows[:, k * LANES : (k + 1) * LANES]
        parts.append(
            (
                jnp.concatenate((column(0), column(2)), axis=0),
                jnp.concatenate((column(1), column(3)), axis=0),
            )
        )
    columns = []
    for j, (re, im) in enumerate(dft4(parts, -1.0)):
        if j:
            cos, sin = turns[0, :, j : j + 1], turns[0, :, 8 + j : 9 + j]
            re, im = re * cos + im * sin, im * cos - re * sin
        columns.append(jnp.concatenate((re, im), axis=0))
    ahead = three(dot, (y_in[0], y_in[1]), split(jnp.concatenate(columns, axis=1)))
    step = plan.major // 4
    scaled = []
    for j in range(4):
        own = ahead[:, j * LANES : (j + 1) * LANES]
        gain = jnp.concatenate([factor[pl.ds((j + 4 * m) * LANES, LANES), :] for m in range(step)], axis=0)
        scaled.append(own * jnp.concatenate((gain, gain), axis=0))
    back = three(dot, (y_out[0], y_out[1]), split(jnp.concatenate(scaled, axis=1)))
    parts = []
    for j in range(4):
        own = back[:, j * LANES : (j + 1) * LANES]
        re, im = own[: plan.quarter], own[plan.quarter :]
        if j:
            cos, sin = turns[1, :, j : j + 1], turns[1, :, 8 + j : 9 + j]
            re, im = re * cos - im * sin, im * cos + re * sin
        parts.append((re, im))
    lines = jnp.concatenate(
        [jnp.concatenate(part, axis=1) for part in dft4(parts, 1.0)], axis=0
    )
    done = three(dot, split(lines), (z_out[0], z_out[1]))
    cos, sin = lane_turn[4:5, :], lane_turn[5:6, :]
    re, im = done[:, :LANES], done[:, LANES:]
    out[:, 0] = (re * cos - im * sin).reshape(plan.n_col, LANES, LANES)
    out[:, 1] = (im * cos + re * sin).reshape(plan.n_col, LANES, LANES)
    for shift in range(plan.n_col):
        outs[shift][...] = out[col ^ shift]


def middle(plan, parts, factor, lane_turn, tables):
    return pl.pallas_call(
        functools.partial(middle_kernel, plan, len(parts)),
        out_shape=[jax.ShapeDtypeStruct((2, LANES, LANES), F32)] * plan.n_col,
        scratch_shapes=[
            pltpu.VMEM((plan.owners, plan.src_rows, LANES), F32),
            pltpu.VMEM((plan.grid // 2, 4 * LANES), F32),
            pltpu.VMEM((plan.n_col, 2, LANES, LANES), F32),
        ],
        compiler_params=pltpu.CompilerParams(vmem_limit_bytes=VMEM_LIMIT),
        name="middle",
    )(*parts, factor, lane_turn, *tables)


def regroup_kernel(plan, *refs):
    parts, outs = refs[: plan.n_row], refs[plan.n_row :]
    for shift in range(plan.n_col):
        for far in range(plan.n_row):
            outs[shift][far] = parts[far][shift]


def regroup(plan, parts):
    return pl.pallas_call(
        functools.partial(regroup_kernel, plan),
        out_shape=[jax.ShapeDtypeStruct((plan.n_row, plan.src_rows, LANES), F32)] * plan.n_col,
        compiler_params=pltpu.CompilerParams(vmem_limit_bytes=VMEM_LIMIT),
        name="regroup",
    )(*parts)


def swap(parts, axis):
    size = len(parts)
    out = [parts[0]] + [None] * (size - 1)
    for shift in reversed(range(1, size)):
        out[shift] = lax.ppermute(parts[shift], axis, [(k, k ^ shift) for k in range(size)])
    return out


def dft(parts, sign):
    size = len(parts)
    if size == 1:
        return parts
    even, odd = dft(parts[0::2], sign), dft(parts[1::2], sign)
    first, second = [], []
    for k in range(size // 2):
        (er, ei), (xr, xi) = even[k], odd[k]
        angle = 2 * math.pi * k / size
        if 4 * k == size:
            xr, xi = -sign * xi, sign * xr
        elif k:
            cos, sin = math.cos(angle), sign * math.sin(angle)
            xr, xi = xr * cos - xi * sin, xr * sin + xi * cos
        first.append((er + xr, ei + xi))
        second.append((er - xr, ei - xi))
    return first + second


def final_kernel(plan, *refs):
    parts, out, got = refs[: plan.n_col], refs[-2], refs[-1]
    scale = 1.0 / (plan.grid * plan.grid)
    col = lax.axis_index("col")
    for shift in range(plan.n_col):
        got[col ^ shift] = parts[shift][...]
    for tile in range(out.shape[1] // 8):
        rows = pl.ds(8 * tile, 8)
        parts = [(got[c, 0, rows, :], got[c, 1, rows, :]) for c in range(plan.n_col)]
        for w, (re, im) in enumerate(dft(parts, 1.0)):
            out[0, rows, pl.ds(w * LANES, LANES)] = re * scale
            out[1, rows, pl.ds(w * LANES, LANES)] = im * scale


FINAL_ROWS = 64


def final(plan, pair, parts, so_far):
    extra = [] if so_far is None else [so_far]
    shape = (plan.planes, LANES, plan.grid)
    return pl.pallas_call(
        functools.partial(final_kernel, plan),
        grid=(LANES // FINAL_ROWS,),
        in_specs=[pl.BlockSpec((2, FINAL_ROWS, LANES), lambda i: (0, i, 0))] * plan.n_col
        + [pl.BlockSpec(memory_space=pl.ANY) for _ in extra],
        out_specs=pl.BlockSpec((2, FINAL_ROWS, plan.grid), lambda i: (pair, i, 0)),
        out_shape=jax.ShapeDtypeStruct(shape, F32),
        scratch_shapes=[pltpu.VMEM((plan.n_col, 2, FINAL_ROWS, LANES), F32)],
        input_output_aliases={plan.n_col: 0} if extra else {},
        compiler_params=pltpu.CompilerParams(vmem_limit_bytes=VMEM_LIMIT),
        name="final",
    )(*parts, *extra)


def lane_turns(plan):
    place, _ = plan.lane_z()
    low = np.stack((place, place + 64, np.arange(LANES))).astype(np.int32)
    phase = lax.axis_index("col") * jnp.asarray(low) % plan.grid
    angle = phase.astype(F32) * (2.0 * math.pi / plan.grid)
    both = jnp.stack((jnp.cos(angle), jnp.sin(angle)), axis=1).reshape(6, LANES)
    return jnp.concatenate((both, jnp.zeros((2, LANES), F32)), axis=0)


def steps(n_row, n_col, top_coeffs, fresh_one, fresh_two, fresh_three, mixing, transfer):
    plan = Plan(n_row, n_col, top_coeffs.shape[1], transfer.shape[0])
    sends = list(expand(plan, top_coeffs, fresh_one, fresh_two, fresh_three, mixing))
    lane_turn = lane_turns(plan)
    y_in, y_out = plan.y_tables()
    tables = [
        jnp.asarray(t)
        for t in (halves(plan.z_table()), halves(y_in), halves(y_out), plan.turns(), halves(plan.z_back()))
    ]
    got = []
    sent = sends[0].reshape(plan.owners, plan.src_rows, LANES)
    got.append([lax.all_to_all(sent, ("row", "col"), split_axis=0, concat_axis=0, tiled=True)])
    if plan.pairs > 1:
        rows = swap([s.reshape(plan.n_col, plan.src_rows, LANES) for s in sends[1:]], "row")
        columns = regroup(plan, rows)
        got.append(swap(columns, "col"))
    result = None
    for pair in range(plan.pairs):
        mid = middle(plan, got[pair], transfer, lane_turn, tables)
        back = swap(mid, "col")
        result = final(plan, pair, back, result)
    return result


def solution(mesh):
    n_row, n_col = mesh.shape["row"], mesh.shape["col"]
    return jax.shard_map(
        functools.partial(steps, n_row, n_col),
        mesh=mesh,
        in_specs=(
            P(None, ("row", "col")),
            P(None, ("row", "col")),
            P(None, None, ("row", "col")),
            P(None, None, ("row", "col")),
            P(),
            P(None, "col"),
        ),
        out_specs=P("row", "col", None),
        check_vma=False,
    )
```

```python
import functools
import math

import jax
import jax.numpy as jnp
import numpy as np
from jax import lax
from jax.experimental import pallas as pl
from jax.experimental.pallas import tpu as pltpu
from jax.sharding import PartitionSpec as P


F32 = jnp.float32
BF16 = jnp.bfloat16
LANES = 128
VMEM_LIMIT = 60 * 1024 * 1024


def bits_of(count):
    return count.bit_length() - 1


class Plan:
    def __init__(self, n_row, n_col, slots, grid):
        self.n_row, self.n_col, self.slots, self.grid = n_row, n_col, slots, grid
        self.owners = n_row * n_col
        self.planes = 16 // n_row
        self.pairs = self.planes // 2
        self.dest_x = n_row // 2
        self.blocks = grid // 8
        self.strip = self.blocks // n_col
        self.inner = slots // (2 * n_col)
        self.major = grid // LANES
        self.quarter = grid // 4
        own_bits = bits_of(self.owners)
        self.own_w = [k for k in range(own_bits) if k % 2 == 0]
        self.own_q = [k for k in range(own_bits) if k % 2 == 1]
        y_bits, z_bits = bits_of(self.strip), bits_of(self.blocks)
        code = []
        for k in range(y_bits):
            code += [("w", k), ("q", k)]
        code += [("w", k) for k in range(y_bits, z_bits)]
        self.inner_bits = code[own_bits:]
        top = bits_of(n_col)
        self.top_w = list(range(z_bits - top, z_bits))
        self.q_in = [k for kind, k in self.inner_bits if kind == "q"]
        self.mid_w = [k for kind, k in self.inner_bits if kind == "w" and k not in self.top_w]
        self.t_low = bits_of(LANES // self.inner)
        self.w_kept = 2 ** len(self.mid_w)
        self.rows_rw = 2 * self.w_kept
        self.small = 2 ** (self.t_low + len(self.q_in))
        assert self.small == 8 and n_col == self.major and slots // 2 == 4 * LANES
        self.src_rows = self.rows_rw * 2 * self.small
        self.group = self.rows_rw * self.small
        self.groups = LANES // self.group
        self.spare = self.groups // 4
        self.own_qs = 2 ** len(self.own_q)
        self.w_extra = 2 ** len(self.own_w) // 8
        assert self.w_extra * self.w_kept == 2
        assert self.pairs in (1, 2)

    def send_table(self):
        lane = np.arange(LANES)
        low_t, inner = lane // self.inner, lane % self.inner
        top = np.zeros(LANES, np.int64)
        small = low_t.copy()
        kept = np.zeros(LANES, np.int64)
        q_value = np.zeros(LANES, np.int64)
        for place, (kind, k) in enumerate(self.inner_bits):
            bit = (inner >> place) & 1
            if kind == "q":
                q_value += bit << self.q_in.index(k)
            elif k in self.top_w:
                top += bit << self.top_w.index(k)
            else:
                kept += bit << self.mid_w.index(k)
        small = (low_t << len(self.q_in)) + q_value
        table = np.zeros((self.n_col, 2, self.w_kept, self.small, 2, LANES))
        for c in range(self.n_col):
            angle = 2 * np.pi * (c * top % self.n_col) / self.n_col
            cos, sin = np.cos(angle), np.sin(angle)
            table[c, 0, kept, small, 0, lane] = cos
            table[c, 0, kept, small, 1, lane] = sin
            table[c, 1, kept, small, 0, lane] = -sin
            table[c, 1, kept, small, 1, lane] = cos
        table = table.reshape(2, self.groups, self.group, 2 * LANES)
        place = np.arange(self.groups)
        turned = np.stack([table[:, place ^ k] for k in range(self.groups)])
        return turned.reshape(self.groups, 2 * LANES, 2 * LANES).transpose(0, 2, 1)

    def lane_z(self):
        lane = np.arange(LANES)
        return (lane >> 4) * 8 + ((lane >> 3) & 1) * 4 + (lane & 3), (lane >> 2) & 1

    def z_table(self):
        low, y_bit = self.lane_z()
        k = np.arange(LANES)
        table = np.zeros((2, 2, LANES, 2, 2, LANES))
        for kept in range(2):
            phase = np.outer(64 * kept + low, k) % LANES
            cos, sin = np.cos(2 * np.pi * phase / LANES), np.sin(2 * np.pi * phase / LANES)
            for b in range(2):
                mask = (y_bit == b)[:, None]
                table[kept, 0, :, b, 0] = cos * mask
                table[kept, 1, :, b, 0] = sin * mask
                table[kept, 0, :, b, 1] = -sin * mask
                table[kept, 1, :, b, 1] = cos * mask
        return table.reshape(4 * LANES, 4 * LANES)

    def y_rows(self):
        y0, own, y21, small = np.indices((2, self.own_qs, 4, self.small))
        n_in = len(self.q_in)
        t_low, q_in = small >> n_in, small & (2 ** n_in - 1)
        q_local = q_in * self.own_qs + own
        return (t_low * LANES + q_local * 8 + y21 * 2 + y0).reshape(-1)

    def m_rows(self):
        step = self.major // 4
        return (np.arange(step)[:, None] + step * np.arange(LANES)[None, :]).reshape(-1)

    def y_tables(self):
        n2, m, size = self.y_rows(), self.m_rows(), self.quarter
        angle = 2 * np.pi * (np.outer(m, n2) % size) / size
        cos, sin = np.cos(angle), np.sin(angle)
        ahead = np.block([[cos, sin], [-sin, cos]])
        angle = 2 * np.pi * (np.outer(np.arange(size), m) % size) / size
        cos, sin = np.cos(angle), np.sin(angle)
        return ahead, np.block([[cos, -sin], [sin, cos]])

    def turns(self):
        out = np.zeros((2, self.quarter, LANES), np.float32)
        for order, n2 in enumerate((self.y_rows(), np.arange(self.quarter))):
            for j in range(4):
                angle = 2 * np.pi * (n2 * j) / self.grid
                out[order, :, j] = np.cos(angle)
                out[order, :, 8 + j] = np.sin(angle)
        return out

    def z_back(self):
        n = np.arange(LANES)
        angle = 2 * np.pi * (np.outer(n, n) % LANES) / LANES
        cos, sin = np.cos(angle), np.sin(angle)
        return np.block([[cos, sin], [-sin, cos]])

    def src(self, w, q):
        index = 0
        for place, bit in enumerate(self.own_w):
            index |= ((w >> place) & 1) << bit
        for place, bit in enumerate(self.own_q):
            index |= ((q >> place) & 1) << bit
        return index


def halves(table):
    high = np.asarray(table, np.float32).astype(BF16)
    low = (np.asarray(table, np.float64) - high.astype(np.float64)).astype(BF16)
    return np.stack((high, low))


def split(x):
    high = x.astype(BF16)
    return high, (x - high.astype(F32)).astype(BF16)


def dot(a, b):
    return jnp.dot(a, b, preferred_element_type=F32)


def three(f, a, b):
    return f(a[0], b[0]) + (f(a[0], b[1]) + f(a[1], b[0]))


def one_hot(shape, hit):
    row = lax.broadcasted_iota(jnp.int32, shape, 0)
    col = lax.broadcasted_iota(jnp.int32, shape, 1)
    return jnp.where(hit(row, col), 1.0, 0.0).astype(BF16)


def widen(table):
    return dot(table, one_hot((64, 448), lambda r, c: r == 8 + c // 8))


def expand_kernel(plan, top, one, two_ref, three_ref, mixing, send_ref, *refs):
    count = plan.pairs if plan.pairs == 1 else plan.n_row + 1
    outs = refs[:count]
    leaf, w_one, w_two, w_three, mine, joined, draws, two, send, read_sem, write_sem = refs[count:]
    my_row, my_col = lax.axis_index("row"), lax.axis_index("col")
    lanes = plan.slots // 2
    reads = [
        pltpu.make_async_copy(three_ref.at[:, :, pl.ds(lanes * half, lanes)], draws.at[half], read_sem.at[half])
        for half in range(2)
    ]
    second_read = pltpu.make_async_copy(two_ref, two, read_sem.at[2])
    table_read = pltpu.make_async_copy(send_ref, send, read_sem.at[3])
    for copy in (second_read, reads[0], table_read, reads[1]):
        copy.start()
    mix = mixing[...]
    child = lambda r: 8 * (4 * (r // 32 % 2) + 2 * (r // 4 % 2) + r % 2)
    cell = lambda r: 4 * (r // 16 % 2) + 2 * (r // 8 % 2) + r // 2 % 2
    picked = dot(one_hot((64, 64), lambda r, c: c == child(r)), mix).astype(BF16)
    row = lax.broadcasted_iota(jnp.int32, (64, 448), 0)
    col = lax.broadcasted_iota(jnp.int32, (64, 448), 1)
    w_three[...] = jnp.where(cell(row) == col % 8, widen(picked), 0.0).astype(BF16)
    last = dot(picked, one_hot((64, 64), lambda r, c: r == c % 8))
    row = lax.broadcasted_iota(jnp.int32, (64, 64), 0)
    col = lax.broadcasted_iota(jnp.int32, (64, 64), 1)
    through = dot(jnp.where(cell(row) == col // 8, last, 0.0).astype(BF16), mix)
    parts = split(through)
    place = lax.broadcasted_iota(jnp.int32, (64, 448), 1) % 8
    for k in range(2):
        wide = widen(parts[k])
        for c in range(8):
            w_two[pl.ds(512 * k + 64 * c, 64), :] = jnp.where(place == c, wide, 0.0).astype(BF16)
    for c in range(8):
        own = mix[8 * c : 8 * c + 8, :]
        table = split(dot(parts[0][:, :8], own) + dot(parts[1][:, :8], own))
        for k in range(2):
            w_one[pl.ds(64 * c, 64), pl.ds(64 * k, 64)] = table[k]
    writes = []
    second_read.wait()
    for half in range(2):
        own = slice(half * lanes, (half + 1) * lanes)
        upper, lower = split(top[:, own])
        ones = jnp.concatenate((upper, one[:, own]), axis=0)
        blocks = jnp.concatenate((ones, ones), axis=0)
        twos = dot(w_two[...], two[:, own])
        second = twos[:512] + (twos[512:] + (dot(w_one[...], blocks) + dot(w_one[:, :8], lower)))
        reads[half].wait()
        for g in range(8):
            fresh = draws[half, :, pl.ds(8 * g, 8), :].reshape(448, lanes)
            leaf[g] = dot(w_three[...], fresh) + second[64 * g : 64 * g + 64]
        if half == 0:
            table_read.wait()
        place = lax.broadcasted_iota(jnp.int32, (plan.src_rows, LANES), 1) // plan.group
        for x2 in range(2):
            made = []
            for k in range(plan.groups):
                spare, tau, high = k // 4, k // 2 % 2, k % 2
                parts = []
                for part in range(2):
                    pieces = []
                    for x1 in range(2):
                        for yz in range(4 // plan.spare):
                            pieces.append(
                                leaf[
                                    4 * x2 + 2 * spare + yz,
                                    pl.ds(32 * part + 16 * x1, 16),
                                    pl.ds((2 * high + tau) * LANES, LANES),
                                ]
                            )
                    parts.append(jnp.concatenate(pieces, axis=0))
                made.append(three(dot, split(jnp.concatenate(parts, axis=1)), (send[0, k], send[1, k])))
            for x1 in range(2):
                x = 2 * x2 + x1
                pair, dest = x % plan.pairs, x // plan.pairs
                for c in range(plan.n_col):
                    side, low = c // plan.groups, c % plan.groups
                    piece = None
                    for k in range(plan.groups):
                        rows = slice(x1 * plan.src_rows, (x1 + 1) * plan.src_rows)
                        own = made[k][rows, side * LANES : (side + 1) * LANES]
                        piece = own if piece is None else jnp.where(place == k ^ low, own, piece)
                    if pair == 0:
                        mine[half, dest, c] = piece
                    else:
                        joined[half * plan.dest_x + dest, c ^ my_col] = piece
        writes.append(pltpu.make_async_copy(mine.at[half], outs[0].at[half], write_sem.at[half]))
        writes[-1].start()
    for far in range(count - 1):
        writes.append(
            pltpu.make_async_copy(joined.at[my_row ^ far], outs[1 + far], write_sem.at[2 + far])
        )
        writes[-1].start()
    for copy in writes:
        copy.wait()


def expand(plan, top, one, two, three_in, mixing):
    lanes = plan.slots // 2
    block = (plan.n_col, plan.src_rows, LANES)
    shapes = [(2, plan.dest_x) + block]
    if plan.pairs > 1:
        shapes += [block] * plan.n_row
    table = halves(plan.send_table())
    inside = pl.BlockSpec(memory_space=pltpu.VMEM)
    outside = pl.BlockSpec(memory_space=pl.ANY)
    return pl.pallas_call(
        functools.partial(expand_kernel, plan),
        in_specs=[inside, inside, outside, outside, inside, outside],
        out_specs=[outside] * len(shapes),
        out_shape=[jax.ShapeDtypeStruct(shape, F32) for shape in shapes],
        scratch_shapes=[
            pltpu.VMEM((8, 64, lanes), F32),
            pltpu.VMEM((512, 128), BF16),
            pltpu.VMEM((1024, 448), BF16),
            pltpu.VMEM((64, 448), BF16),
            pltpu.VMEM(shapes[0], F32),
            pltpu.VMEM((plan.n_row,) + block, F32),
            pltpu.VMEM((2, 56, 64, lanes), BF16),
            pltpu.VMEM((448, plan.slots), BF16),
            pltpu.VMEM(table.shape, BF16),
            pltpu.SemaphoreType.DMA((4,)),
            pltpu.SemaphoreType.DMA((2 + plan.n_row,)),
        ],
        compiler_params=pltpu.CompilerParams(vmem_limit_bytes=VMEM_LIMIT),
        name="expand",
    )(top, one, two.reshape(448, plan.slots), three_in, mixing, jnp.asarray(table))


def dft4(parts, sign):
    (ar, ai), (br, bi), (cr, ci), (dr, di) = parts
    pr, pi, mr, mi = ar + cr, ai + ci, ar - cr, ai - ci
    qr, qi, nr, ni = br + dr, bi + di, br - dr, bi - di
    return [
        (pr + qr, pi + qi),
        (mr - sign * ni, mi + sign * nr),
        (pr - qr, pi - qi),
        (mr + sign * ni, mi - sign * nr),
    ]


def middle_kernel(plan, count, *refs):
    parts, refs = refs[:count], refs[count:]
    factor, lane_turn, z_in, y_in, y_out, turns, z_out = refs[:7]
    outs = refs[7 : 7 + plan.n_col]
    got, prep, out = refs[7 + plan.n_col :]
    row, col = lax.axis_index("row"), lax.axis_index("col")
    if count == 1:
        got = parts[0]
    else:
        for shift in range(plan.n_col):
            for far in range(plan.n_row):
                got[(row ^ far) * plan.n_col + (col ^ shift)] = parts[shift][far]
    q_tiles = plan.own_qs * 4
    for q in range(plan.own_qs):
        for extra in range(plan.w_extra):
            for y21 in range(4 // plan.spare):
                y2, y1 = y21 // 2, y21 % 2
                pieces = [
                    got[plan.src(extra * 8 + w, q), pl.ds(8 * (4 * y2 + 2 * z2 + y1), 8), :]
                    for w in range(8)
                    for z2 in range(2)
                ]
                block = jnp.concatenate(pieces, axis=0).T
                block = block.reshape(plan.groups, 2, plan.w_kept, 8, LANES)
                for kept_in in range(plan.w_kept):
                    kept = extra if plan.w_extra == 2 else kept_in
                    cos = lane_turn[2 * kept : 2 * kept + 1, :]
                    sin = lane_turn[2 * kept + 1 : 2 * kept + 2, :]
                    for k in range(plan.groups):
                        re, im = block[k, 0, kept_in], block[k, 1, kept_in]
                        own = k ^ (col & (plan.groups - 1))
                        spare, tau, high = own >> 2, (own >> 1) & 1, own & 1
                        tile = (2 * high + tau) * q_tiles + q * 4 + spare * 2 + y21
                        rows = pl.ds(pl.multiple_of(8 * tile, 8), 8)
                        prep[rows, pl.ds(2 * kept * LANES, LANES)] = re * cos + im * sin
                        prep[rows, pl.ds((2 * kept + 1) * LANES, LANES)] = im * cos - re * sin
    z_done = three(dot, split(prep[...]), (z_in[0], z_in[1]))
    size = 8 * q_tiles
    parts = []
    for tile in range(4):
        rows = z_done[tile * size : (tile + 1) * size]
        column = lambda k: rows[:, k * LANES : (k + 1) * LANES]
        parts.append(
            (
                jnp.concatenate((column(0), column(2)), axis=0),
                jnp.concatenate((column(1), column(3)), axis=0),
            )
        )
    columns = []
    for j, (re, im) in enumerate(dft4(parts, -1.0)):
        if j:
            cos, sin = turns[0, :, j : j + 1], turns[0, :, 8 + j : 9 + j]
            re, im = re * cos + im * sin, im * cos - re * sin
        columns.append(jnp.concatenate((re, im), axis=0))
    ahead = three(dot, (y_in[0], y_in[1]), split(jnp.concatenate(columns, axis=1)))
    step = plan.major // 4
    scaled = []
    for j in range(4):
        own = ahead[:, j * LANES : (j + 1) * LANES]
        gain = jnp.concatenate([factor[pl.ds((j + 4 * m) * LANES, LANES), :] for m in range(step)], axis=0)
        scaled.append(own * jnp.concatenate((gain, gain), axis=0))
    back = three(dot, (y_out[0], y_out[1]), split(jnp.concatenate(scaled, axis=1)))
    parts = []
    for j in range(4):
        own = back[:, j * LANES : (j + 1) * LANES]
        re, im = own[: plan.quarter], own[plan.quarter :]
        if j:
            cos, sin = turns[1, :, j : j + 1], turns[1, :, 8 + j : 9 + j]
            re, im = re * cos - im * sin, im * cos + re * sin
        parts.append((re, im))
    lines = jnp.concatenate(
        [jnp.concatenate(part, axis=1) for part in dft4(parts, 1.0)], axis=0
    )
    done = three(dot, split(lines), (z_out[0], z_out[1]))
    cos, sin = lane_turn[4:5, :], lane_turn[5:6, :]
    re, im = done[:, :LANES], done[:, LANES:]
    out[:, 0] = (re * cos - im * sin).reshape(plan.n_col, LANES, LANES)
    out[:, 1] = (im * cos + re * sin).reshape(plan.n_col, LANES, LANES)
    for shift in range(plan.n_col):
        outs[shift][...] = out[col ^ shift]


def middle(plan, parts, factor, lane_turn, tables):
    return pl.pallas_call(
        functools.partial(middle_kernel, plan, len(parts)),
        out_shape=[jax.ShapeDtypeStruct((2, LANES, LANES), F32)] * plan.n_col,
        scratch_shapes=[
            pltpu.VMEM((plan.owners, plan.src_rows, LANES), F32),
            pltpu.VMEM((plan.grid // 2, 4 * LANES), F32),
            pltpu.VMEM((plan.n_col, 2, LANES, LANES), F32),
        ],
        compiler_params=pltpu.CompilerParams(vmem_limit_bytes=VMEM_LIMIT),
        name="middle",
    )(*parts, factor, lane_turn, *tables)


def regroup_kernel(plan, *refs):
    parts, outs = refs[: plan.n_row], refs[plan.n_row :]
    for shift in range(plan.n_col):
        for far in range(plan.n_row):
            outs[shift][far] = parts[far][shift]


def regroup(plan, parts):
    return pl.pallas_call(
        functools.partial(regroup_kernel, plan),
        out_shape=[jax.ShapeDtypeStruct((plan.n_row, plan.src_rows, LANES), F32)] * plan.n_col,
        compiler_params=pltpu.CompilerParams(vmem_limit_bytes=VMEM_LIMIT),
        name="regroup",
    )(*parts)


def swap(parts, axis):
    size = len(parts)
    out = [parts[0]] + [None] * (size - 1)
    for shift in reversed(range(1, size)):
        out[shift] = lax.ppermute(parts[shift], axis, [(k, k ^ shift) for k in range(size)])
    return out


def dft(parts, sign):
    size = len(parts)
    if size == 1:
        return parts
    even, odd = dft(parts[0::2], sign), dft(parts[1::2], sign)
    first, second = [], []
    for k in range(size // 2):
        (er, ei), (xr, xi) = even[k], odd[k]
        angle = 2 * math.pi * k / size
        if 4 * k == size:
            xr, xi = -sign * xi, sign * xr
        elif k:
            cos, sin = math.cos(angle), sign * math.sin(angle)
            xr, xi = xr * cos - xi * sin, xr * sin + xi * cos
        first.append((er + xr, ei + xi))
        second.append((er - xr, ei - xi))
    return first + second


def final_kernel(plan, *refs):
    parts, out, got = refs[: plan.n_col], refs[-2], refs[-1]
    scale = 1.0 / (plan.grid * plan.grid)
    col = lax.axis_index("col")
    for shift in range(plan.n_col):
        got[col ^ shift] = parts[shift][...]
    for tile in range(out.shape[1] // 8):
        rows = pl.ds(8 * tile, 8)
        parts = [(got[c, 0, rows, :], got[c, 1, rows, :]) for c in range(plan.n_col)]
        for w, (re, im) in enumerate(dft(parts, 1.0)):
            out[0, rows, pl.ds(w * LANES, LANES)] = re * scale
            out[1, rows, pl.ds(w * LANES, LANES)] = im * scale


FINAL_ROWS = 64


def final(plan, pair, parts, so_far):
    extra = [] if so_far is None else [so_far]
    shape = (plan.planes, LANES, plan.grid)
    return pl.pallas_call(
        functools.partial(final_kernel, plan),
        grid=(LANES // FINAL_ROWS,),
        in_specs=[pl.BlockSpec((2, FINAL_ROWS, LANES), lambda i: (0, i, 0))] * plan.n_col
        + [pl.BlockSpec(memory_space=pl.ANY) for _ in extra],
        out_specs=pl.BlockSpec((2, FINAL_ROWS, plan.grid), lambda i: (pair, i, 0)),
        out_shape=jax.ShapeDtypeStruct(shape, F32),
        scratch_shapes=[pltpu.VMEM((plan.n_col, 2, FINAL_ROWS, LANES), F32)],
        input_output_aliases={plan.n_col: 0} if extra else {},
        compiler_params=pltpu.CompilerParams(vmem_limit_bytes=VMEM_LIMIT),
        name="final",
    )(*[pltpu.with_memory_space_constraint(part, pltpu.HBM) for part in parts], *extra)


def lane_turns(plan):
    place, _ = plan.lane_z()
    low = np.stack((place, place + 64, np.arange(LANES))).astype(np.int32)
    phase = lax.axis_index("col") * jnp.asarray(low) % plan.grid
    angle = phase.astype(F32) * (2.0 * math.pi / plan.grid)
    both = jnp.stack((jnp.cos(angle), jnp.sin(angle)), axis=1).reshape(6, LANES)
    return jnp.concatenate((both, jnp.zeros((2, LANES), F32)), axis=0)


def steps(n_row, n_col, top_coeffs, fresh_one, fresh_two, fresh_three, mixing, transfer):
    plan = Plan(n_row, n_col, top_coeffs.shape[1], transfer.shape[0])
    sends = list(expand(plan, top_coeffs, fresh_one, fresh_two, fresh_three, mixing))
    lane_turn = lane_turns(plan)
    y_in, y_out = plan.y_tables()
    tables = [
        jnp.asarray(t)
        for t in (halves(plan.z_table()), halves(y_in), halves(y_out), plan.turns(), halves(plan.z_back()))
    ]
    got = []
    sent = sends[0].reshape(plan.owners, plan.src_rows, LANES)
    got.append([lax.all_to_all(sent, ("row", "col"), split_axis=0, concat_axis=0, tiled=True)])
    if plan.pairs > 1:
        rows = swap([s.reshape(plan.n_col, plan.src_rows, LANES) for s in sends[1:]], "row")
        columns = regroup(plan, rows)
        got.append(swap(columns, "col"))
    result = None
    for pair in range(plan.pairs):
        mid = middle(plan, got[pair], transfer, lane_turn, tables)
        back = swap(mid, "col")
        result = final(plan, pair, back, result)
    return result


def solution(mesh):
    n_row, n_col = mesh.shape["row"], mesh.shape["col"]
    return jax.shard_map(
        functools.partial(steps, n_row, n_col),
        mesh=mesh,
        in_specs=(
            P(None, ("row", "col")),
            P(None, ("row", "col")),
            P(None, None, ("row", "col")),
            P(None, None, ("row", "col")),
            P(),
            P(None, "col"),
        ),
        out_specs=P("row", "col", None),
        check_vma=False,
    )
```
